512 devices in a mesh: rep: 4 (over y), exp: 128 (over x, z, core).
Axes of the slice: x: 4, y: 4, z: 16, core: 2. Of those that a mesh axis runs over, the one named last changes fastest.
Arguments:
- tokens: bfloat16 [16384, 3584], P(('rep', 'exp')), parts along dimension 0, may hold values from -6 to 6
- expert_ids: int32 [16384, 8], P(('rep', 'exp')), parts along dimension 0, may hold values from 0 to 383, all different within a row; in each aligned block of 32 rows (0 to 31, 32 to 63, ...) at most 2 rows name the same one
- gate_scores: float32 [16384, 8], P(('rep', 'exp')), parts along dimension 0, may hold values from 0.02 to 0.4
- gate_weight: bfloat16 [3584, 16384], P(None, 'exp'), may hold values from -0.09375 to 0.09375
- up_weight: bfloat16 [3584, 16384], P(None, 'exp'), may hold values from -0.09375 to 0.09375
- down_weight: bfloat16 [16384, 3584], P('exp'), may hold values from -0.125 to 0.125
Outputs:
- combined: bfloat16 [16384, 3584], P(('rep', 'exp')), parts along dimension 0
- expert_load: float32 [1536], P('rep'), parts along dimension 0
The draws below stay inside these ranges and needn't reach their ends.
There are 4 independent parts, one for each index of `rep`. The reference program is written for one: setup_inputs(seed, part) draws one part's arguments, and reference() takes and returns one part's arrays. A program takes and returns all parts, laid end to end along the dimension named above; an argument that names none is the same for every part. Nothing has to cross between parts.
Inputs may be any that keep to these rules, and one draw needn't show every extreme that they name: `expert_ids`: each row names 8 different experts. Among the rows of one device no expert is named by more than 2 rows, a bound that some block reaches.
All inputs are finite; a program needn't handle non-finite values.
Results may differ from the reference program's by a relative error of at most 0.0057.
Values may be sent and summed in bfloat16 or wider, within the bound.
No kernel may reach another device: no remote copies, remote signals or barrier semaphores. Data moves between devices by JAX's collectives and lax.ppermute only.
A program may use at most 64 MiB of HBM per device.

```python
import math
import jax
import jax.numpy as jnp
import numpy as np

D = 3584
FF = 2048
EXPERTS_ALL = 384
TOP = 8
EXPERTS = 8
TOK_DEV = 32
CAP = 2
HID_DEV = 128
TOKENS = 4096
N_EXP = 128


def levels(rng, shape, cuts, low, largest):
    gain = 1.0
    for position, parts in cuts:
        heights = jax.random.uniform(jax.random.fold_in(jax.random.fold_in(rng, 6), position), (parts,), jnp.float32, low / len(cuts), largest / len(cuts))
        gain = gain * jnp.repeat(jnp.exp(heights), shape[position] // parts).reshape((-1,) + (1,) * (len(shape) - 1 - position))
    return gain


def assign_block(stream_key, own, number, rows, amount, top, reach, slope):
    ranking = jax.random.permutation(stream_key, amount)
    crowded, common = portions_of(amount, rows * top, reach, slope, True), portions_of(amount, rows * top, reach, slope, False)
    places = jnp.arange(amount)

    def named(tallies, rotation):
        used = int((tallies > 0).sum())
        fixed = max(1, used // 4)
        shifted = fixed + (places - fixed + rotation * (used - fixed)) % max(1, amount - fixed)
        return jnp.zeros((amount,), jnp.int32).at[ranking[jnp.where(places < fixed, places, shifted)]].set(jnp.asarray(tallies, jnp.int32))

    tallies = jnp.where(number % 4 == 0, named(crowded, number // 4), named(common, number - number // 4 - 1))
    mixed = jax.random.permutation(jax.random.fold_in(own, 3), amount)
    giver, receiver = mixed[0:amount // 2 * 2:2], mixed[1:amount // 2 * 2:2]
    slack = jnp.minimum(tallies[giver] - 1, reach - tallies[receiver]) // 2
    slack = jnp.where((giver == ranking[0]) | (receiver == ranking[0]) | (tallies[receiver] == 0), 0, jnp.maximum(slack, 0))
    shifted = jax.random.randint(jax.random.fold_in(own, 4), (amount // 2,), 0, 1 << 20) % (slack + 1)
    tallies = tallies.at[giver].add(-shifted).at[receiver].add(shifted)
    labels = jnp.searchsorted(jnp.cumsum(tallies), jnp.arange(rows * top), side="right").astype(jnp.int32)
    grid = labels.reshape(top, rows).T
    grid = grid[jax.random.permutation(jax.random.fold_in(own, 1), rows)]
    rotation = jax.random.randint(jax.random.fold_in(own, 2), (rows, 1), 0, top)
    return jnp.take_along_axis(grid, (jnp.arange(top)[None, :] + rotation) % top, axis=1)


def portions_of(amount, total, limit, slope, full):
    loads = [(1 << 20) // math.isqrt(standing ** slope) + 1 for standing in range(1, amount + 1)]
    largest = limit if full else min(limit, max(-(-total // amount), total * loads[0] // sum(loads)))
    least = 1 if total - largest >= amount - 1 else 0
    holding, rest = [largest] + [least] * (amount - 1), total - largest - least * (amount - 1)
    while rest > 0:
        movable = [i for i in range(1, amount) if holding[i] < largest] or [i for i in range(1, amount) if holding[i] < limit]
        mass, budget = sum([loads[i] for i in movable]), rest
        for i in movable:
            addition = min(limit - holding[i], max(1, budget * loads[i] // mass), rest)
            holding[i] = holding[i] + addition
            rest = rest - addition
    return np.array(holding)


def noise(own_key, dims, deviation, limit, split=(), kind=jnp.bfloat16):
    values = jax.random.normal(own_key, dims, jnp.float32) * deviation
    if len(split) > 0:
        values = levels(own_key, dims, split, -0.22, 0.18) * values
    return jnp.clip(values, min=-limit, max=limit).astype(kind)


def setup_inputs(seed: int = 0, part: int = 0) -> dict:
    seeds = jax.random.split(jax.random.key(seed), 7)
    own_keys = jax.random.split(jax.random.fold_in(seeds[6], part), 7)
    tokens = noise(own_keys[0], (TOKENS, D), 1.0, 6.0, ((0, 128),))
    expert_ids_keys = jax.random.split(jax.random.fold_in(own_keys[1], 1), TOKENS // TOK_DEV)
    expert_ids_turns = jax.random.permutation(jax.random.fold_in(own_keys[1], 3), TOKENS // TOK_DEV)
    expert_ids = jax.vmap(lambda own, number: assign_block(jax.random.fold_in(own_keys[1], 2), own, number, TOK_DEV, EXPERTS_ALL, TOP, CAP, 1))(expert_ids_keys, expert_ids_turns).reshape((TOKENS, TOP))
    gate_scores = jnp.clip(jnp.exp(math.log(0.4) - 2.9957323 * jax.random.uniform(own_keys[2], (TOKENS, TOP), jnp.float32) ** levels(own_keys[2], (TOKENS, TOP), ((0, 128),), -0.2, 0.2)), 0.02, 0.4)
    gate_weight = noise(seeds[3], (D, EXPERTS * FF), D ** -0.5, 0.09375, ((1, 128),))
    up_weight = noise(seeds[4], (D, EXPERTS * FF), D ** -0.5, 0.09375, ((1, 128),))
    down_weight = noise(seeds[5], (EXPERTS * FF, D), FF ** -0.5, 0.125, ((0, 128),))
    return {"tokens": tokens, "expert_ids": expert_ids, "gate_scores": gate_scores, "gate_weight": gate_weight, "up_weight": up_weight, "down_weight": down_weight}


def reference(tokens, expert_ids, gate_scores, gate_weight, up_weight, down_weight):
    expert_load = jax.ops.segment_sum(gate_scores.reshape(-1), expert_ids.reshape(-1).astype(jnp.int32), num_segments=EXPERTS_ALL)
    rows_bound = N_EXP * CAP
    combined_sum = jnp.zeros((TOKENS, D), jnp.float32)
    for expert in range(EXPERTS):
        matches = expert_ids == expert
        row_gate = jnp.sum(jnp.where(matches, gate_scores, 0.0), axis=1)
        named = jnp.any(matches, axis=1)
        chosen = jnp.nonzero(named, size=rows_bound, fill_value=0)[0].astype(jnp.int32)
        is_live = jnp.arange(rows_bound, dtype=jnp.int32) < jnp.sum(named.astype(jnp.int32))
        picked = tokens[chosen]
        first = expert * FF
        gate_act = jnp.dot(picked, gate_weight[:, first:first + FF], preferred_element_type=jnp.float32)
        up_act = jnp.dot(picked, up_weight[:, first:first + FF], preferred_element_type=jnp.float32)
        hidden = (jax.nn.silu(gate_act) * up_act).astype(jnp.bfloat16)
        result = jnp.zeros((rows_bound, D), jnp.float32)
        for block_index in range(FF // HID_DEV):
            low = block_index * HID_DEV
            partial_value = jnp.dot(hidden[:, low:low + HID_DEV], down_weight[first + low:first + low + HID_DEV, :], preferred_element_type=jnp.float32).astype(jnp.bfloat16)
            result = result + partial_value.astype(jnp.float32)
        row_scale = jnp.where(is_live, row_gate[chosen], 0.0)
        combined_sum = combined_sum.at[chosen].add(row_scale[:, None] * result)
    return combined_sum.astype(jnp.bfloat16), expert_load
```

```python
import jax
import jax.numpy as jnp
from jax import lax
from jax.sharding import PartitionSpec as P

EXPERTS_ALL = 384
EXPERTS = 8
CAP = 2
COLS, RINGS, CORES = 4, 16, 2
PAIRS = RINGS // 2


def place(col, ring, core):
    return (col * RINGS + ring) * CORES + core


def far_groups():
    groups = []
    for side in range(2):
        for core in range(CORES):
            groups.append(
                [
                    place(col, 2 * pair + (side if pair < PAIRS // 2 else 1 - side), core)
                    for col in range(COLS)
                    for pair in range(PAIRS)
                ]
            )
    return groups


FAR = far_groups()
MEMBERS = COLS * PAIRS
SPREAD = MEMBERS // EXPERTS
BESIDE = [(i, i ^ CORES) for i in range(COLS * RINGS * CORES)]
TWIN = [(i, i ^ 1) for i in range(COLS * RINGS * CORES)]
SLICE = EXPERTS_ALL // MEMBERS


def split3(v):
    a = v.astype(jnp.bfloat16)
    r = v - a.astype(jnp.float32)
    b = r.astype(jnp.bfloat16)
    c = (r - b.astype(jnp.float32)).astype(jnp.bfloat16)
    return a, b, c


def shards(tokens, expert_ids, gate_scores, gate_weight, up_weight, down_weight):
    bf, f32 = jnp.bfloat16, jnp.float32
    tok_rows, width = tokens.shape
    weights = (gate_weight, up_weight, down_weight)
    twins = tuple(lax.ppermute(w, "exp", TWIN) for w in weights)

    matches = expert_ids[:, :, None] == jnp.arange(EXPERTS_ALL, dtype=jnp.int32)[None, None, :]
    onehot = jnp.where(matches, 1.0, 0.0).astype(f32)
    mass = jnp.einsum("tk,tke->e", gate_scores, onehot, precision=lax.Precision.HIGHEST)
    window = matches[:, :, :EXPERTS]
    hits = jnp.any(window, axis=1)
    gate = jnp.sum(jnp.where(window, gate_scores[:, :, None], 0.0), axis=1)
    lower = (jnp.arange(tok_rows)[:, None] >= jnp.arange(tok_rows)[None, :]).astype(bf)
    position = jnp.dot(lower, hits.astype(bf), preferred_element_type=f32).astype(jnp.int32) - 1
    slots = jnp.arange(CAP, dtype=jnp.int32)
    placed = hits[:, :, None] & (position[:, :, None] == slots[None, None, :])
    placing = placed.reshape(tok_rows, EXPERTS * CAP)
    picker = jnp.where(placing.T, 1.0, 0.0).astype(bf)
    out = jnp.dot(picker, tokens, preferred_element_type=f32).astype(bf)
    out = jnp.broadcast_to(out.reshape(EXPERTS, 1, CAP, width), (EXPERTS, SPREAD, CAP, width))
    out = out.reshape(MEMBERS, CAP, width)
    mass = lax.psum(lax.psum(lax.psum(mass, "exp", axis_index_groups=CG), "exp", axis_index_groups=XG), "exp", axis_index_groups=ZG)
    arrived = lax.all_to_all(out, "exp", 0, 0, axis_index_groups=FAR, tiled=True)
    mine = arrived.reshape(MEMBERS * CAP, width)
    theirs = lax.ppermute(mine, "exp", BESIDE)

    def expert(rows):
        total = 0.0
        for gw, uw, dw in zip(*((w, t) for w, t in zip(weights, twins))):
            g = jnp.dot(rows, gw, preferred_element_type=f32)
            u = jnp.dot(rows, uw, preferred_element_type=f32)
            h = (jax.nn.silu(g) * u).astype(bf)
            total = total + jnp.dot(h, dw, preferred_element_type=f32)
        return total

    back = lax.ppermute(expert(theirs).astype(bf), "exp", BESIDE)
    both = (expert(mine) + back.astype(f32)).astype(bf).reshape(MEMBERS, CAP, width)
    returned = lax.all_to_all(both, "exp", 0, 0, axis_index_groups=FAR, tiled=True)
    summed = jnp.sum(returned.reshape(EXPERTS, SPREAD, CAP, width), axis=1, dtype=f32)
    scale = jnp.where(placed, gate[:, :, None], 0.0).reshape(tok_rows, EXPERTS * CAP)
    combined = jnp.dot(scale, summed.reshape(EXPERTS * CAP, width), precision=lax.Precision.HIGHEST)
    return combined.astype(bf), mass


CG = [[place(c, r, k) for k in range(CORES)] for c in range(COLS) for r in range(RINGS)]
XG = [[place(c, r, k) for c in range(COLS)] for r in range(RINGS) for k in range(CORES)]
ZG = [[place(c, r, k) for r in range(RINGS)] for c in range(COLS) for k in range(CORES)]


def solution(mesh):
    return jax.shard_map(
        shards,
        mesh=mesh,
        in_specs=(
            P(("rep", "exp"), None),
            P(("rep", "exp"), None),
            P(("rep", "exp"), None),
            P(None, "exp"),
            P(None, "exp"),
            P("exp", None),
        ),
        out_specs=(P(("rep", "exp"), None), P("rep")),
        check_vma=False,
    )
```

```python
import jax
import jax.numpy as jnp
from jax import lax
from jax.sharding import PartitionSpec as P

EXPERTS_ALL = 384
EXPERTS = 8
CAP = 2
COLS, RINGS, CORES = 4, 16, 2
PAIRS = RINGS // 2


def place(col, ring, core):
    return (col * RINGS + ring) * CORES + core


def far_groups():
    groups = []
    for side in range(2):
        for core in range(CORES):
            groups.append(
                [
                    place(col, 2 * pair + (side if pair < PAIRS // 2 else 1 - side), core)
                    for col in range(COLS)
                    for pair in range(PAIRS)
                ]
            )
    return groups


FAR = far_groups()
MEMBERS = COLS * PAIRS
SPREAD = MEMBERS // EXPERTS
BESIDE = [(i, i ^ CORES) for i in range(COLS * RINGS * CORES)]
TWIN = [(i, i ^ 1) for i in range(COLS * RINGS * CORES)]
SLICE = EXPERTS_ALL // MEMBERS
RIDER = 128


def split3(v):
    a = v.astype(jnp.bfloat16)
    r = v - a.astype(jnp.float32)
    b = r.astype(jnp.bfloat16)
    c = (r - b.astype(jnp.float32)).astype(jnp.bfloat16)
    return a, b, c


def riders(slices):
    row = jnp.concatenate(split3(slices), axis=1)
    return jnp.pad(row[:, None, :], ((0, 0), (0, CAP - 1), (0, RIDER - 3 * SLICE)))


def shards(tokens, expert_ids, gate_scores, gate_weight, up_weight, down_weight):
    bf, f32 = jnp.bfloat16, jnp.float32
    tok_rows, width = tokens.shape
    weights = (gate_weight, up_weight, down_weight)
    twins = tuple(lax.ppermute(w, "exp", TWIN) for w in weights)

    matches = expert_ids[:, :, None] == jnp.arange(EXPERTS_ALL, dtype=jnp.int32)[None, None, :]
    onehot = jnp.where(matches, 1.0, 0.0).astype(f32)
    mass = jnp.einsum("tk,tke->e", gate_scores, onehot, precision=lax.Precision.HIGHEST)
    window = matches[:, :, :EXPERTS]
    hits = jnp.any(window, axis=1)
    gate = jnp.sum(jnp.where(window, gate_scores[:, :, None], 0.0), axis=1)
    lower = (jnp.arange(tok_rows)[:, None] >= jnp.arange(tok_rows)[None, :]).astype(bf)
    position = jnp.dot(lower, hits.astype(bf), preferred_element_type=f32).astype(jnp.int32) - 1
    slots = jnp.arange(CAP, dtype=jnp.int32)
    placed = hits[:, :, None] & (position[:, :, None] == slots[None, None, :])
    placing = placed.reshape(tok_rows, EXPERTS * CAP)
    picker = jnp.where(placing.T, 1.0, 0.0).astype(bf)
    out = jnp.dot(picker, tokens, preferred_element_type=f32).astype(bf)
    out = jnp.broadcast_to(out.reshape(EXPERTS, 1, CAP, width), (EXPERTS, SPREAD, CAP, width))
    out = out.reshape(MEMBERS, CAP, width)
    out = jnp.concatenate([out, riders(mass.reshape(MEMBERS, SLICE))], axis=2)
    arrived = lax.all_to_all(out, "exp", 0, 0, axis_index_groups=FAR, tiled=True)
    mine = arrived.reshape(MEMBERS * CAP, width + RIDER)
    theirs = lax.ppermute(mine, "exp", BESIDE)
    part = jnp.sum(mine[:, width:], axis=0, dtype=f32) + jnp.sum(theirs[:, width:], axis=0, dtype=f32)
    part = jnp.sum(part[: 3 * SLICE].reshape(3, SLICE), axis=0, keepdims=True)
    part = part + lax.ppermute(part, "exp", TWIN)
    mine, theirs = mine[:, :width], theirs[:, :width]

    def expert(rows):
        total = 0.0
        for gw, uw, dw in zip(*((w, t) for w, t in zip(weights, twins))):
            g = jnp.dot(rows, gw, preferred_element_type=f32)
            u = jnp.dot(rows, uw, preferred_element_type=f32)
            h = (jax.nn.silu(g) * u).astype(bf)
            total = total + jnp.dot(h, dw, preferred_element_type=f32)
        return total

    back = lax.ppermute(expert(theirs).astype(bf), "exp", BESIDE)
    both = (expert(mine) + back.astype(f32)).astype(bf).reshape(MEMBERS, CAP, width)
    both = jnp.concatenate([both, riders(jnp.broadcast_to(part, (MEMBERS, SLICE)))], axis=2)
    returned = lax.all_to_all(both, "exp", 0, 0, axis_index_groups=FAR, tiled=True)
    mass = jnp.sum(returned[:, 0, width : width + 3 * SLICE].astype(f32).reshape(MEMBERS, 3, SLICE), axis=1).reshape(-1)
    summed = jnp.sum(returned[:, :, :width].reshape(EXPERTS, SPREAD, CAP, width), axis=1, dtype=f32)
    scale = jnp.where(placed, gate[:, :, None], 0.0).reshape(tok_rows, EXPERTS * CAP)
    combined = jnp.dot(scale, summed.reshape(EXPERTS * CAP, width), precision=lax.Precision.HIGHEST)
    return combined.astype(bf), mass


def solution(mesh):
    return jax.shard_map(
        shards,
        mesh=mesh,
        in_specs=(
            P(("rep", "exp"), None),
            P(("rep", "exp"), None),
            P(("rep", "exp"), None),
            P(None, "exp"),
            P(None, "exp"),
            P("exp", None),
        ),
        out_specs=(P(("rep", "exp"), None), P("rep")),
        check_vma=False,
    )
```

```python
import functools

import jax
import jax.numpy as jnp
from jax import lax
from jax.experimental import pallas as pl
from jax.experimental.pallas import tpu as pltpu
from jax.sharding import PartitionSpec as P

EXPERTS_ALL = 384
EXPERTS = 8
CAP = 2
COLS, RINGS, CORES = 4, 16, 2
PAIRS = RINGS // 2
CHUNKS = 1
F32, BF16, I32 = jnp.float32, jnp.bfloat16, jnp.int32


def place(col, ring, core):
    return (col * RINGS + ring) * CORES + core


def far_groups():
    groups = []
    for side in range(2):
        for core in range(CORES):
            members = []
            for col in range(COLS):
                for spot in range(PAIRS):
                    pair = (spot + 6 + 4 * side) % PAIRS
                    ring = 2 * pair + (side if pair < PAIRS // 2 else 1 - side)
                    members.append(place(col, ring, core))
            groups.append(members)
    return groups


FAR = far_groups()
MEMBERS = COLS * PAIRS
SPREAD = MEMBERS // EXPERTS
ROWS = MEMBERS * CAP
BESIDE = [(i, i ^ CORES) for i in range(COLS * RINGS * CORES)]
TWIN = [(i, i ^ 1) for i in range(COLS * RINGS * CORES)]
SLICE = EXPERTS_ALL // MEMBERS
RIDER = 128


def split3(v):
    a = v.astype(BF16)
    r = v - a.astype(F32)
    b = r.astype(BF16)
    c = (r - b.astype(F32)).astype(BF16)
    return a, b, c


def by_slice(e):
    return (e * 171) >> 11


def expert_of(member, side):
    spot = member & (PAIRS - 1)
    inner = (spot >= 2) & (spot < 6)
    return 2 * (member >> 3) + jnp.where(inner, side, 1 - side)


def slice_of(member, side):
    return (member & ~(PAIRS - 1)) + ((member + 6 + 4 * side) & (PAIRS - 1))


def iota(shape, axis):
    return lax.broadcasted_iota(I32, shape, axis)


def whole():
    return pl.BlockSpec(memory_space=pltpu.VMEM)


def scalar():
    return pl.BlockSpec(memory_space=pltpu.SMEM)


def pack_kernel(side_ref, tok_hbm, ids_ref, score_ref, out_ref, scale_ref, tok_ref, flip_ids, flip_score, sem):
    fetch = pltpu.make_async_copy(tok_hbm, tok_ref, sem)
    fetch.start()
    side = side_ref[0]
    rows, width = tok_ref.shape
    top = ids_ref.shape[0]
    flip_ids[...] = jnp.zeros_like(flip_ids)
    flip_score[...] = jnp.zeros_like(flip_score)
    flip_ids[:top, :rows] = ids_ref[...]
    flip_score[:top, :rows] = score_ref[...]
    ids, score = flip_ids[...].T[:rows], flip_score[...].T[:rows]
    every = iota((rows, EXPERTS_ALL), 1)
    column = iota((rows, 128), 1)
    named = jnp.where(column < ROWS, expert_of(column >> 1, side), -1)
    mass = jnp.zeros((rows, EXPERTS_ALL), F32)
    gate = jnp.zeros((rows, 128), F32)
    hit = jnp.zeros((rows, 128), F32)
    for k in range(top):
        one, s = ids[:, k : k + 1], score[:, k : k + 1]
        mass = mass + jnp.where(every == one, s, 0.0)
        same = named == one
        gate = gate + jnp.where(same, s, 0.0)
        hit = hit + jnp.where(same, 1.0, 0.0)
    lower = jnp.where(iota((rows, rows), 0) >= iota((rows, rows), 1), 1.0, 0.0)
    rank = jnp.dot(lower.astype(BF16), hit.astype(BF16), preferred_element_type=F32) - 1.0
    slot = (column & 1).astype(F32)
    placed = (hit > 0.5) & (rank == slot)
    scale = split3(jnp.where(placed, gate, 0.0))
    for i, part in enumerate(scale):
        scale_ref[i * rows : (i + 1) * rows, :] = part
    pick = jnp.where(placed, 1.0, 0.0).T[:ROWS].astype(BF16)
    fetch.wait()
    out_ref[:, :width] = jnp.dot(pick, tok_ref[...], preferred_element_type=F32).astype(BF16)
    load = jnp.sum(mass, axis=0, keepdims=True)
    row, e = iota((ROWS, EXPERTS_ALL), 0), iota((ROWS, EXPERTS_ALL), 1)
    mine = ((row & 1) == 0) & (slice_of(row >> 1, side) == by_slice(e))
    e2, lane = iota((EXPERTS_ALL, RIDER), 0), iota((EXPERTS_ALL, RIDER), 1)
    within = e2 - SLICE * by_slice(e2)
    rider = jnp.zeros((ROWS, RIDER), F32)
    for i, term in enumerate(split3(load)):
        spread = jnp.where(mine, term.astype(F32), 0.0).astype(BF16)
        select = jnp.where(lane == within + i * SLICE, 1.0, 0.0).astype(BF16)
        rider = rider + jnp.dot(spread, select, preferred_element_type=F32)
    out_ref[:, width:] = rider.astype(BF16)


def pack(side, tokens, ids, scores):
    rows, width = tokens.shape
    return pl.pallas_call(
        pack_kernel,
        out_shape=(
            jax.ShapeDtypeStruct((ROWS, width + RIDER), BF16),
            jax.ShapeDtypeStruct((3 * rows, 128), BF16),
        ),
        in_specs=[scalar(), pl.BlockSpec(memory_space=pl.ANY), whole(), whole()],
        out_specs=(whole(), whole()),
        scratch_shapes=[
            pltpu.VMEM((rows, width), BF16),
            pltpu.VMEM((128, 128), I32),
            pltpu.VMEM((128, 128), F32),
            pltpu.SemaphoreType.DMA(()),
        ],
        compiler_params=pltpu.CompilerParams(vmem_limit_bytes=6 << 20),
        name="pack",
    )(side, tokens, ids.T, scores.T)


def expert_kernel(x_ref, *refs):
    hbm, (out_ref, wide, down, sems) = refs[:6], refs[6:]
    width, hid = hbm[0].shape
    targets = [wide.at[i] for i in range(4)] + [down.at[pl.ds(i * hid, hid), :] for i in range(2)]
    copies = [pltpu.make_async_copy(ref, buf, sems.at[i]) for i, (ref, buf) in enumerate(zip(hbm, targets))]
    for copy in copies:
        copy.start()
    x = x_ref[:, :width]
    act = []
    for i in range(4):
        copies[i].wait()
        act.append(jnp.dot(x, wide[i], preferred_element_type=F32))
    g = jnp.concatenate(act[:2], axis=1)
    u = jnp.concatenate(act[2:], axis=1)
    h = (g / (1.0 + jnp.exp(-g)) * u).astype(BF16)
    copies[4].wait()
    copies[5].wait()
    out_ref[...] = jnp.dot(h, down[...], preferred_element_type=F32).astype(out_ref.dtype)


def expert(x, weights, twins, dtype):
    rows = x.shape[0]
    width, hid = weights[0].shape
    operands = [w for pair in zip(weights, twins) for w in pair]
    return pl.pallas_call(
        expert_kernel,
        out_shape=jax.ShapeDtypeStruct((rows, width), dtype),
        in_specs=[whole()] + [pl.BlockSpec(memory_space=pl.ANY)] * 6,
        out_specs=whole(),
        scratch_shapes=[
            pltpu.VMEM((4, width, hid), BF16),
            pltpu.VMEM((2 * hid, width), BF16),
            pltpu.SemaphoreType.DMA((6,)),
        ],
        cost_estimate=pl.CostEstimate(
            flops=12 * rows * width * hid, bytes_accessed=12 * width * hid, transcendentals=rows * 2 * hid
        ),
        compiler_params=pltpu.CompilerParams(vmem_limit_bytes=12 << 20),
        name="expert",
    )(x, *operands)


def join_kernel(own_ref, rider_ref, *refs):
    backs, out_ref = refs[:-1], refs[-1]
    width = own_ref.shape[1]
    first = 0
    for back in backs:
        span = pl.ds(first, back.shape[0])
        out_ref[span, :width] = (own_ref[span, :] + back[...].astype(F32)).astype(BF16)
        first += back.shape[0]
    even = (iota((ROWS, RIDER), 0) & 1) == 0
    out_ref[:, width:] = jnp.where(even, rider_ref[...], 0.0).astype(BF16)


def join(own, rider, backs):
    return pl.pallas_call(
        join_kernel,
        out_shape=jax.ShapeDtypeStruct((ROWS, own.shape[1] + RIDER), BF16),
        in_specs=[whole()] * (2 + len(backs)),
        out_specs=whole(),
        compiler_params=pltpu.CompilerParams(vmem_limit_bytes=6 << 20),
        name="join",
    )(own, rider, *backs)


def combine_kernel(side_ref, rows_ref, scale_ref, out_ref, mass_ref):
    side = side_ref[0]
    tok, width = out_ref.shape
    weight = scale_ref[:, :ROWS]
    parts = jnp.dot(weight, rows_ref[:, :width], preferred_element_type=F32)
    out_ref[...] = (parts[:tok] + parts[tok : 2 * tok] + parts[2 * tok :]).astype(BF16)
    lane, e = iota((RIDER, EXPERTS_ALL), 0), iota((RIDER, EXPERTS_ALL), 1)
    within = e - SLICE * by_slice(e)
    same = (lane == within) | (lane == within + SLICE) | (lane == within + 2 * SLICE)
    total = jnp.dot(rows_ref[:, width:], jnp.where(same, 1.0, 0.0).astype(BF16), preferred_element_type=F32)
    row, e2 = iota((ROWS, EXPERTS_ALL), 0), iota((ROWS, EXPERTS_ALL), 1)
    mine = ((row & 1) == 0) & (slice_of(row >> 1, side) == by_slice(e2))
    mass_ref[...] = jnp.sum(jnp.where(mine, total, 0.0), axis=0)


def combine(side, rows, scale, tok):
    width = rows.shape[1] - RIDER
    return pl.pallas_call(
        combine_kernel,
        out_shape=(jax.ShapeDtypeStruct((tok, width), BF16), jax.ShapeDtypeStruct((EXPERTS_ALL,), F32)),
        in_specs=[scalar(), whole(), whole()],
        out_specs=(whole(), whole()),
        compiler_params=pltpu.CompilerParams(vmem_limit_bytes=6 << 20),
        name="combine",
    )(side, rows, scale)


def far(rows):
    blocks = rows.reshape(MEMBERS, CAP, rows.shape[1])
    return lax.all_to_all(blocks, "exp", 0, 0, axis_index_groups=FAR, tiled=True).reshape(rows.shape)


def shards(tokens, expert_ids, gate_scores, gate_weight, up_weight, down_weight):
    tok_rows, width = tokens.shape
    weights = (gate_weight, up_weight, down_weight)
    twins = tuple(lax.ppermute(w, "exp", TWIN) for w in weights)
    ring = (lax.axis_index("exp") // CORES) % RINGS
    side = ((ring & 1) ^ (ring >> 3)).astype(I32).reshape(1)
    out, scale = pack(side, tokens, expert_ids, gate_scores)
    mine = far(out)
    step = ROWS // CHUNKS
    theirs = [lax.ppermute(mine[i * step : (i + 1) * step], "exp", BESIDE) for i in range(CHUNKS)]
    own = expert(mine, weights, twins, F32)
    partials = [expert(x, weights, twins, BF16) for x in theirs]
    backs = [lax.ppermute(p, "exp", BESIDE) for p in partials]
    part = sum(jnp.sum(x[:, width:], axis=0, dtype=F32) for x in [mine] + theirs)
    part = jnp.sum(part[: 3 * SLICE].reshape(3, SLICE), axis=0, keepdims=True)
    part, _ = lax.optimization_barrier((part, partials[-1]))
    part = part + lax.ppermute(part, "exp", TWIN)
    rider = jnp.concatenate([t.astype(F32) for t in split3(part)], axis=1)
    rider = jnp.pad(rider, ((0, 0), (0, RIDER - 3 * SLICE)))
    returned = far(join(own, rider, backs))
    combined, mass = combine(side, returned, scale, tok_rows)
    return combined, mass


def solution(mesh):
    return jax.shard_map(
        shards,
        mesh=mesh,
        in_specs=(
            P(("rep", "exp"), None),
            P(("rep", "exp"), None),
            P(("rep", "exp"), None),
            P(None, "exp"),
            P(None, "exp"),
            P("exp", None),
        ),
        out_specs=(P(("rep", "exp"), None), P("rep")),
        check_vma=False,
    )
```

```python
import functools

import jax
import jax.numpy as jnp
from jax import lax
from jax.experimental import pallas as pl
from jax.experimental.pallas import tpu as pltpu
from jax.sharding import PartitionSpec as P

EXPERTS_ALL = 384
EXPERTS = 8
CAP = 2
COLS, RINGS, CORES = 4, 16, 2
PAIRS = RINGS // 2
CHUNKS = 2
F32, BF16, I32 = jnp.float32, jnp.bfloat16, jnp.int32


def place(col, ring, core):
    return (col * RINGS + ring) * CORES + core


def far_groups():
    groups = []
    for side in range(2):
        for core in range(CORES):
            members = []
            for col in range(COLS):
                for spot in range(PAIRS):
                    pair = (spot + 6 + 4 * side) % PAIRS
                    ring = 2 * pair + (side if pair < PAIRS // 2 else 1 - side)
                    members.append(place(col, ring, core))
            groups.append(members)
    return groups


FAR = far_groups()
MEMBERS = COLS * PAIRS
SPREAD = MEMBERS // EXPERTS
ROWS = MEMBERS * CAP
BESIDE = [(i, i ^ CORES) for i in range(COLS * RINGS * CORES)]
TWIN = [(i, i ^ 1) for i in range(COLS * RINGS * CORES)]
SLICE = EXPERTS_ALL // MEMBERS
RIDER = 128
TERMS = 3 * SLICE


def split3(v):
    a = v.astype(BF16)
    r = v - a.astype(F32)
    b = r.astype(BF16)
    c = (r - b.astype(F32)).astype(BF16)
    return a, b, c


def by_slice(e):
    return (e * 171) >> 11


def expert_of(member, side):
    spot = member & (PAIRS - 1)
    inner = (spot >= 2) & (spot < 6)
    return 2 * (member >> 3) + jnp.where(inner, side, 1 - side)


def slice_of(member, side):
    return (member & ~(PAIRS - 1)) + ((member + 6 + 4 * side) & (PAIRS - 1))


def iota(shape, axis):
    return lax.broadcasted_iota(I32, shape, axis)


def whole():
    return pl.BlockSpec(memory_space=pltpu.VMEM)


def scalar():
    return pl.BlockSpec(memory_space=pltpu.SMEM)


def pack_kernel(side_ref, tok_hbm, ids_ref, score_ref, out_ref, scale_ref, tok_ref, flip_ids, flip_score, sem):
    fetch = pltpu.make_async_copy(tok_hbm, tok_ref, sem)
    fetch.start()
    side = side_ref[0]
    rows, width = tok_ref.shape
    top = ids_ref.shape[0]
    flip_ids[...] = jnp.zeros_like(flip_ids)
    flip_score[...] = jnp.zeros_like(flip_score)
    flip_ids[:top, :rows] = ids_ref[...]
    flip_score[:top, :rows] = score_ref[...]
    ids, score = flip_ids[...].T[:rows], flip_score[...].T[:rows]
    every = iota((rows, EXPERTS_ALL), 1)
    column = iota((rows, 128), 1)
    named = jnp.where(column < ROWS, expert_of(column >> 1, side), -1)
    mass = jnp.zeros((rows, EXPERTS_ALL), F32)
    gate = jnp.zeros((rows, 128), F32)
    hit = jnp.zeros((rows, 128), F32)
    for k in range(top):
        one, s = ids[:, k : k + 1], score[:, k : k + 1]
        mass = mass + jnp.where(every == one, s, 0.0)
        same = named == one
        gate = gate + jnp.where(same, s, 0.0)
        hit = hit + jnp.where(same, 1.0, 0.0)
    lower = jnp.where(iota((rows, rows), 0) >= iota((rows, rows), 1), 1.0, 0.0)
    rank = jnp.dot(lower.astype(BF16), hit.astype(BF16), preferred_element_type=F32) - 1.0
    slot = (column & 1).astype(F32)
    placed = (hit > 0.5) & (rank == slot)
    scale = split3(jnp.where(placed, gate, 0.0))
    for i, part in enumerate(scale):
        scale_ref[i * rows : (i + 1) * rows, :] = part
    pick = jnp.where(placed, 1.0, 0.0).T[:ROWS].astype(BF16)
    fetch.wait()
    picked = jnp.dot(pick, tok_ref[...], preferred_element_type=F32).astype(BF16)
    out_ref[:, :, :width] = picked.reshape(MEMBERS, CAP, width)
    load = jnp.sum(mass, axis=0, keepdims=True)
    row, e = iota((ROWS, EXPERTS_ALL), 0), iota((ROWS, EXPERTS_ALL), 1)
    mine = ((row & 1) == 0) & (slice_of(row >> 1, side) == by_slice(e))
    e2, lane = iota((EXPERTS_ALL, RIDER), 0), iota((EXPERTS_ALL, RIDER), 1)
    within = e2 - SLICE * by_slice(e2)
    rider = jnp.zeros((ROWS, RIDER), F32)
    for i, term in enumerate(split3(load)):
        spread = jnp.where(mine, term.astype(F32), 0.0).astype(BF16)
        select = jnp.where(lane == within + i * SLICE, 1.0, 0.0).astype(BF16)
        rider = rider + jnp.dot(spread, select, preferred_element_type=F32)
    out_ref[:, :, width:] = rider.astype(BF16).reshape(MEMBERS, CAP, RIDER)


def pack(side, tokens, ids, scores):
    rows, width = tokens.shape
    return pl.pallas_call(
        pack_kernel,
        out_shape=(
            jax.ShapeDtypeStruct((MEMBERS, CAP, width + RIDER), BF16),
            jax.ShapeDtypeStruct((3 * rows, 128), BF16),
        ),
        in_specs=[scalar(), pl.BlockSpec(memory_space=pl.ANY), whole(), whole()],
        out_specs=(whole(), whole()),
        scratch_shapes=[
            pltpu.VMEM((rows, width), BF16),
            pltpu.VMEM((128, 128), I32),
            pltpu.VMEM((128, 128), F32),
            pltpu.SemaphoreType.DMA(()),
        ],
        compiler_params=pltpu.CompilerParams(vmem_limit_bytes=6 << 20),
        name="pack",
    )(side, tokens, ids.T, scores.T)


def expert_kernel(n_sums, x_ref, *refs):
    sums, hbm, (out_ref, sum_ref, wide, down, sems) = refs[:n_sums], refs[n_sums : n_sums + 6], refs[n_sums + 6 :]
    width, hid = hbm[0].shape
    targets = [wide.at[i] for i in range(4)] + [down.at[pl.ds(i * hid, hid), :] for i in range(2)]
    copies = [pltpu.make_async_copy(ref, buf, sems.at[i]) for i, (ref, buf) in enumerate(zip(hbm, targets))]
    for copy in copies:
        copy.start()
    rows = x_ref[...].reshape(-1, x_ref.shape[-1])
    x = rows[:, :width]
    total = jnp.sum(rows[:, width:].astype(F32), axis=0, keepdims=True)
    for other in sums:
        total = total + other[...]
    sum_ref[...] = total
    act = []
    for i in range(4):
        copies[i].wait()
        act.append(jnp.dot(x, wide[i], preferred_element_type=F32))
    g = jnp.concatenate(act[:2], axis=1)
    u = jnp.concatenate(act[2:], axis=1)
    h = (g / (1.0 + jnp.exp(-g)) * u).astype(BF16)
    copies[4].wait()
    copies[5].wait()
    out_ref[...] = jnp.dot(h, down[...], preferred_element_type=F32).astype(out_ref.dtype)


def expert(x, sums, weights, twins, dtype):
    rows = x.shape[0] * CAP
    width, hid = weights[0].shape
    operands = [w for pair in zip(weights, twins) for w in pair]
    return pl.pallas_call(
        functools.partial(expert_kernel, len(sums)),
        out_shape=(jax.ShapeDtypeStruct((rows, width), dtype), jax.ShapeDtypeStruct((1, RIDER), F32)),
        in_specs=[whole()] * (1 + len(sums)) + [pl.BlockSpec(memory_space=pl.ANY)] * 6,
        out_specs=(whole(), whole()),
        scratch_shapes=[
            pltpu.VMEM((4, width, hid), BF16),
            pltpu.VMEM((2 * hid, width), BF16),
            pltpu.SemaphoreType.DMA((6,)),
        ],
        compiler_params=pltpu.CompilerParams(vmem_limit_bytes=14 << 20),
        cost_estimate=pl.CostEstimate(
            flops=12 * rows * width * hid, bytes_accessed=12 * width * hid, transcendentals=rows * 2 * hid
        ),
        name="expert",
    )(x, *sums, *operands)


def join_kernel(own_ref, sum_ref, twin_ref, *refs):
    backs, out_ref = refs[:-1], refs[-1]
    width = own_ref.shape[1]
    first = 0
    for back in backs:
        many = back.shape[0]
        both = (own_ref[pl.ds(first, many), :] + back[...].astype(F32)).astype(BF16)
        out_ref[pl.ds(first // CAP, many // CAP), :, :width] = both.reshape(many // CAP, CAP, width)
        first += many
    shape = (ROWS, RIDER)
    value = jnp.broadcast_to(sum_ref[...] + twin_ref[...], shape)
    keep = ((iota(shape, 0) & 1) == 0) & (iota(shape, 1) < TERMS)
    rider = jnp.zeros(shape, F32)
    for i, term in enumerate(split3(value)):
        term = jnp.where(keep, term.astype(F32), 0.0)
        rider = rider + (pltpu.roll(term, i * TERMS, 1) if i else term)
    out_ref[:, :, width:] = rider.astype(BF16).reshape(MEMBERS, CAP, RIDER)


def join(own, total, twin, backs):
    return pl.pallas_call(
        join_kernel,
        out_shape=jax.ShapeDtypeStruct((MEMBERS, CAP, own.shape[1] + RIDER), BF16),
        in_specs=[whole()] * (3 + len(backs)),
        out_specs=whole(),
        compiler_params=pltpu.CompilerParams(vmem_limit_bytes=8 << 20),
        name="join",
    )(own, total, twin, *backs)


def combine_kernel(side_ref, rows_ref, scale_ref, out_ref, mass_ref):
    side = side_ref[0]
    tok, width = out_ref.shape
    weight = scale_ref[:, :ROWS]
    rows = rows_ref[...].reshape(ROWS, -1)
    parts = jnp.dot(weight, rows[:, :width], preferred_element_type=F32)
    out_ref[...] = (parts[:tok] + parts[tok : 2 * tok] + parts[2 * tok :]).astype(BF16)
    lane, e = iota((RIDER, EXPERTS_ALL), 0), iota((RIDER, EXPERTS_ALL), 1)
    within = e - SLICE * by_slice(e)
    same = (lane - SLICE * by_slice(lane) == within) & (lane < 3 * TERMS)
    total = jnp.dot(rows[:, width:], jnp.where(same, 1.0, 0.0).astype(BF16), preferred_element_type=F32)
    row, e2 = iota((ROWS, EXPERTS_ALL), 0), iota((ROWS, EXPERTS_ALL), 1)
    mine = ((row & 1) == 0) & (slice_of(row >> 1, side) == by_slice(e2))
    mass_ref[...] = jnp.sum(jnp.where(mine, total, 0.0), axis=0)


def combine(side, rows, scale, tok):
    width = rows.shape[2] - RIDER
    return pl.pallas_call(
        combine_kernel,
        out_shape=(jax.ShapeDtypeStruct((tok, width), BF16), jax.ShapeDtypeStruct((EXPERTS_ALL,), F32)),
        in_specs=[scalar(), whole(), whole()],
        out_specs=(whole(), whole()),
        compiler_params=pltpu.CompilerParams(vmem_limit_bytes=6 << 20),
        name="combine",
    )(side, rows, scale)


def far(blocks):
    return lax.all_to_all(blocks, "exp", 0, 0, axis_index_groups=FAR, tiled=True)


def shards(tokens, expert_ids, gate_scores, gate_weight, up_weight, down_weight):
    tok_rows, width = tokens.shape
    weights = (gate_weight, up_weight, down_weight)
    twins = tuple(lax.ppermute(w, "exp", TWIN) for w in weights)
    ring = (lax.axis_index("exp") // CORES) % RINGS
    side = ((ring & 1) ^ (ring >> 3)).astype(I32).reshape(1)
    out, scale = pack(side, tokens, expert_ids, gate_scores)
    mine = far(out)
    step = MEMBERS // CHUNKS
    theirs = [lax.ppermute(mine[i * step : (i + 1) * step], "exp", BESIDE) for i in range(CHUNKS)]
    backs, total = [], []
    for x in theirs:
        partial, summed = expert(x, total, weights, twins, BF16)
        backs.append(lax.ppermute(partial, "exp", BESIDE))
        total = [summed]
    own, total = expert(mine, total, weights, twins, F32)
    returned = far(join(own, total, lax.ppermute(total, "exp", TWIN), backs))
    combined, mass = combine(side, returned, scale, tok_rows)
    return combined, mass


def solution(mesh):
    return jax.shard_map(
        shards,
        mesh=mesh,
        in_specs=(
            P(("rep", "exp"), None),
            P(("rep", "exp"), None),
            P(("rep", "exp"), None),
            P(None, "exp"),
            P(None, "exp"),
            P("exp", None),
        ),
        out_specs=(P(("rep", "exp"), None), P("rep")),
        check_vma=False,
    )
```

```python
import functools

import jax
import jax.numpy as jnp
from jax import lax
from jax.experimental import pallas as pl
from jax.experimental.pallas import tpu as pltpu
from jax.sharding import PartitionSpec as P


EXPERTS_ALL = 384
CAP = 2
COLS, RINGS, CORES = 4, 16, 2
PAIRS = RINGS // 2
CHUNKS = 2
F32, BF16, I32 = jnp.float32, jnp.bfloat16, jnp.int32


def place(col, ring, core):
    return (col * RINGS + ring) * CORES + core


def far_groups():
    groups = []
    for side in range(2):
        for core in range(CORES):
            members = []
            for col in range(COLS):
                for spot in range(PAIRS):
                    pair = (spot + 6 + 4 * side) % PAIRS
                    ring = 2 * pair + (side if pair < PAIRS // 2 else 1 - side)
                    members.append(place(col, ring, core))
            groups.append(members)
    return groups


FAR = far_groups()
MEMBERS = COLS * PAIRS
ROWS = MEMBERS * CAP
BESIDE = [(i, i ^ CORES) for i in range(COLS * RINGS * CORES)]
TWIN = [(i, i ^ 1) for i in range(COLS * RINGS * CORES)]
SLICE = EXPERTS_ALL // MEMBERS
RIDER = 128
TERMS = 3 * SLICE


def split3(v):
    a = v.astype(BF16)
    r = v - a.astype(F32)
    b = r.astype(BF16)
    c = (r - b.astype(F32)).astype(BF16)
    return a, b, c


def by_slice(e):
    return (e * 171) >> 11


def expert_of(member, side):
    spot = member & (PAIRS - 1)
    inner = (spot >= 2) & (spot < 6)
    return 2 * (member >> 3) + jnp.where(inner, side, 1 - side)


def slice_of(member, side):
    return (member & ~(PAIRS - 1)) + ((member + 6 + 4 * side) & (PAIRS - 1))


def iota(shape, axis):
    return lax.broadcasted_iota(I32, shape, axis)


def whole():
    return pl.BlockSpec(memory_space=pltpu.VMEM)


def scalar():
    return pl.BlockSpec(memory_space=pltpu.SMEM)


def pack_kernel(side_ref, tok_hbm, ids_hbm, score_hbm, out_ref, scale_ref, tok_ref, ids_ref, score_ref, flip_ids, flip_score, sems):
    fetch = pltpu.make_async_copy(tok_hbm, tok_ref, sems.at[0])
    small = [
        pltpu.make_async_copy(ids_hbm, ids_ref, sems.at[1]),
        pltpu.make_async_copy(score_hbm, score_ref, sems.at[2]),
    ]
    for copy in small + [fetch]:
        copy.start()
    side = side_ref[0]
    rows, width = tok_ref.shape
    top = ids_ref.shape[0]
    flip_ids[...] = jnp.zeros_like(flip_ids)
    flip_score[...] = jnp.zeros_like(flip_score)
    for copy in small:
        copy.wait()
    flip_ids[:top, :rows] = ids_ref[...]
    flip_score[:top, :rows] = score_ref[...]
    ids, score = flip_ids[...].T[:rows], flip_score[...].T[:rows]
    every = iota((rows, EXPERTS_ALL), 1)
    column = iota((rows, 128), 1)
    named = jnp.where(column < ROWS, expert_of(column >> 1, side), -1)
    mass = jnp.zeros((rows, EXPERTS_ALL), F32)
    gate = jnp.zeros((rows, 128), F32)
    hit = jnp.zeros((rows, 128), F32)
    for k in range(top):
        one, s = ids[:, k : k + 1], score[:, k : k + 1]
        mass = mass + jnp.where(every == one, s, 0.0)
        same = named == one
        gate = gate + jnp.where(same, s, 0.0)
        hit = hit + jnp.where(same, 1.0, 0.0)
    lower = jnp.where(iota((rows, rows), 0) >= iota((rows, rows), 1), 1.0, 0.0)
    rank = jnp.dot(lower.astype(BF16), hit.astype(BF16), preferred_element_type=F32) - 1.0
    slot = (column & 1).astype(F32)
    placed = (hit > 0.5) & (rank == slot)
    scale = split3(jnp.where(placed, gate, 0.0))
    for i, part in enumerate(scale):
        scale_ref[i * rows : (i + 1) * rows, :] = part
    pick = jnp.where(placed, 1.0, 0.0).T[:ROWS].astype(BF16)
    fetch.wait()
    picked = jnp.dot(pick, tok_ref[...], preferred_element_type=F32).astype(BF16)
    out_ref[:, :, :width] = picked.reshape(MEMBERS, CAP, width)
    load = jnp.sum(mass, axis=0, keepdims=True)
    row, e = iota((ROWS, EXPERTS_ALL), 0), iota((ROWS, EXPERTS_ALL), 1)
    mine = ((row & 1) == 0) & (slice_of(row >> 1, side) == by_slice(e))
    e2, lane = iota((EXPERTS_ALL, RIDER), 0), iota((EXPERTS_ALL, RIDER), 1)
    within = e2 - SLICE * by_slice(e2)
    rider = jnp.zeros((ROWS, RIDER), F32)
    for i, term in enumerate(split3(load)):
        spread = jnp.where(mine, term.astype(F32), 0.0).astype(BF16)
        select = jnp.where(lane == within + i * SLICE, 1.0, 0.0).astype(BF16)
        rider = rider + jnp.dot(spread, select, preferred_element_type=F32)
    out_ref[:, :, width:] = rider.astype(BF16).reshape(MEMBERS, CAP, RIDER)


def pack(side, tokens, ids, scores):
    rows, width = tokens.shape
    return pl.pallas_call(
        pack_kernel,
        out_shape=(
            jax.ShapeDtypeStruct((MEMBERS, CAP, width + RIDER), BF16),
            jax.ShapeDtypeStruct((3 * rows, 128), BF16),
        ),
        in_specs=[scalar()] + [pl.BlockSpec(memory_space=pl.ANY)] * 3,
        out_specs=(whole(), whole()),
        scratch_shapes=[
            pltpu.VMEM((rows, width), BF16),
            pltpu.VMEM(ids.shape[::-1], I32),
            pltpu.VMEM(scores.shape[::-1], F32),
            pltpu.VMEM((128, 128), I32),
            pltpu.VMEM((128, 128), F32),
            pltpu.SemaphoreType.DMA((3,)),
        ],
        compiler_params=pltpu.CompilerParams(vmem_limit_bytes=60 << 20),
        name="pack",
    )(side, tokens, ids.T, scores.T)


def expert_kernel(n_sums, x_ref, *refs):
    sums, mats, (out_ref, sum_ref) = refs[:n_sums], refs[n_sums : n_sums + 6], refs[n_sums + 6 :]
    width, hid = mats[0].shape
    rows = x_ref[...].reshape(-1, x_ref.shape[-1])
    x = rows[:, :width]
    total = jnp.sum(rows[:, width:].astype(F32), axis=0, keepdims=True)
    for other in sums:
        if other.shape[0] == 1:
            total = total + other[...]
        else:
            more = other[...].reshape(-1, other.shape[-1])[:, width:]
            total = total + jnp.sum(more.astype(F32), axis=0, keepdims=True)
    sum_ref[...] = total
    act = []
    for i in range(4):
        act.append(jnp.dot(x, mats[i][...], preferred_element_type=F32))
    g = jnp.concatenate(act[:2], axis=1)
    u = jnp.concatenate(act[2:], axis=1)
    h = (g / (1.0 + jnp.exp(-g)) * u).astype(BF16)
    out = [jnp.dot(h[:, i * hid : (i + 1) * hid], mats[4 + i][...], preferred_element_type=F32) for i in range(2)]
    out_ref[...] = (out[0] + out[1]).astype(out_ref.dtype)


def expert(x, sums, weights, twins, dtype):
    rows = x.shape[0] * CAP
    width, hid = weights[0].shape
    operands = [w for pair in zip(weights, twins) for w in pair]
    return pl.pallas_call(
        functools.partial(expert_kernel, len(sums)),
        out_shape=(jax.ShapeDtypeStruct((rows, width), dtype), jax.ShapeDtypeStruct((1, RIDER), F32)),
        in_specs=[whole()] * (7 + len(sums)),
        out_specs=(whole(), whole()),
        compiler_params=pltpu.CompilerParams(vmem_limit_bytes=14 << 20),
        cost_estimate=pl.CostEstimate(
            flops=12 * rows * width * hid, bytes_accessed=12 * width * hid, transcendentals=rows * 2 * hid
        ),
        name="expert",
    )(x, *sums, *operands)


def hold_kernel(*refs):
    n = len(refs) // 2
    sems = refs[-1]
    copies = [pltpu.make_async_copy(refs[i], refs[n + i], sems.at[i]) for i in range(n)]
    for copy in copies:
        copy.start()
    for copy in copies:
        copy.wait()


def hold(weights):
    return pl.pallas_call(
        hold_kernel,
        out_shape=tuple(jax.ShapeDtypeStruct(w.shape, w.dtype) for w in weights),
        in_specs=[pl.BlockSpec(memory_space=pl.ANY)] * len(weights),
        out_specs=(whole(),) * len(weights),
        scratch_shapes=[pltpu.SemaphoreType.DMA((len(weights),))],
        compiler_params=pltpu.CompilerParams(vmem_limit_bytes=4 << 20),
        name="hold",
    )(*weights)


def cut_kernel(whole_ref, *part_refs):
    many = part_refs[0].shape[0]
    for i, part in enumerate(part_refs):
        part[...] = whole_ref[pl.ds(i * many, many)]


def cut(blocks, pieces):
    shape = (blocks.shape[0] // pieces,) + blocks.shape[1:]
    return pl.pallas_call(
        cut_kernel,
        out_shape=(jax.ShapeDtypeStruct(shape, blocks.dtype),) * pieces,
        in_specs=[whole()],
        out_specs=(whole(),) * pieces,
        compiler_params=pltpu.CompilerParams(vmem_limit_bytes=3 << 20),
        name="cut",
    )(blocks)


def join_kernel(own_ref, sum_ref, twin_ref, *refs):
    backs, out_ref = refs[:-1], refs[-1]
    width = own_ref.shape[1]
    first = 0
    for back in backs:
        many = back.shape[0]
        both = (own_ref[pl.ds(first, many), :] + back[...].astype(F32)).astype(BF16)
        out_ref[pl.ds(first // CAP, many // CAP), :, :width] = both.reshape(many // CAP, CAP, width)
        first += many
    shape = (ROWS, RIDER)
    value = jnp.broadcast_to(sum_ref[...] + twin_ref[...], shape)
    keep = ((iota(shape, 0) & 1) == 0) & (iota(shape, 1) < TERMS)
    rider = jnp.zeros(shape, F32)
    for i, term in enumerate(split3(value)):
        term = jnp.where(keep, term.astype(F32), 0.0)
        rider = rider + (pltpu.roll(term, i * TERMS, 1) if i else term)
    out_ref[:, :, width:] = rider.astype(BF16).reshape(MEMBERS, CAP, RIDER)


def join(own, total, twin, backs):
    return pl.pallas_call(
        join_kernel,
        out_shape=jax.ShapeDtypeStruct((MEMBERS, CAP, own.shape[1] + RIDER), BF16),
        in_specs=[whole()] * (3 + len(backs)),
        out_specs=whole(),
        compiler_params=pltpu.CompilerParams(vmem_limit_bytes=8 << 20),
        name="join",
    )(own, total, twin, *backs)


def combine_kernel(side_ref, rows_ref, scale_ref, out_ref, mass_ref):
    side = side_ref[0]
    tok, width = out_ref.shape
    weight = scale_ref[:, :ROWS]
    rows = rows_ref[...].reshape(ROWS, -1)
    parts = jnp.dot(weight, rows[:, :width], preferred_element_type=F32)
    out_ref[...] = (parts[:tok] + parts[tok : 2 * tok] + parts[2 * tok :]).astype(BF16)
    lane, e = iota((RIDER, EXPERTS_ALL), 0), iota((RIDER, EXPERTS_ALL), 1)
    within = e - SLICE * by_slice(e)
    same = (lane - SLICE * by_slice(lane) == within) & (lane < 3 * TERMS)
    total = jnp.dot(rows[:, width:], jnp.where(same, 1.0, 0.0).astype(BF16), preferred_element_type=F32)
    row, e2 = iota((ROWS, EXPERTS_ALL), 0), iota((ROWS, EXPERTS_ALL), 1)
    mine = ((row & 1) == 0) & (slice_of(row >> 1, side) == by_slice(e2))
    mass_ref[...] = jnp.sum(jnp.where(mine, total, 0.0), axis=0)


def combine(side, rows, scale, tok):
    width = rows.shape[2] - RIDER
    return pl.pallas_call(
        combine_kernel,
        out_shape=(jax.ShapeDtypeStruct((tok, width), BF16), jax.ShapeDtypeStruct((EXPERTS_ALL,), F32)),
        in_specs=[scalar(), whole(), whole()],
        out_specs=(whole(), whole()),
        compiler_params=pltpu.CompilerParams(vmem_limit_bytes=6 << 20),
        name="combine",
    )(side, rows, scale)


def far(blocks):
    return lax.all_to_all(blocks, "exp", 0, 0, axis_index_groups=FAR, tiled=True)


def shards(tokens, expert_ids, gate_scores, gate_weight, up_weight, down_weight):
    tok_rows, _ = tokens.shape
    weights = (gate_weight, up_weight, down_weight)
    twins = tuple(lax.ppermute(w, "exp", TWIN) for w in weights)
    ring = (lax.axis_index("exp") // CORES) % RINGS
    side = ((ring & 1) ^ (ring >> 3)).astype(I32).reshape(1)
    out, scale = pack(side, tokens, expert_ids, gate_scores)
    mine = far(out)
    held = hold(weights)
    theirs = []
    for piece in cut(mine, CHUNKS):
        theirs.append(lax.ppermute(piece, "exp", BESIDE))
    backs, total = [], []
    for i, x in enumerate(theirs):
        partial, summed = expert(x, total + [mine] * (i == CHUNKS - 1), held, twins, BF16)
        backs.append(lax.ppermute(partial, "exp", BESIDE))
        total = [summed]
    own, _ = expert(mine, [], held, twins, F32)
    other = lax.ppermute(total[0], "exp", TWIN)
    returned = far(join(own, total[0], other, backs))
    combined, mass = combine(side, returned, scale, tok_rows)
    return combined, mass


def solution(mesh):
    return jax.shard_map(
        shards,
        mesh=mesh,
        in_specs=(
            P(("rep", "exp"), None),
            P(("rep", "exp"), None),
            P(("rep", "exp"), None),
            P(None, "exp"),
            P(None, "exp"),
            P("exp", None),
        ),
        out_specs=(P(("rep", "exp"), None), P("rep")),
        check_vma=False,
    )
```

```python
import functools

import jax
import jax.numpy as jnp
from jax import lax
from jax.experimental import pallas as pl
from jax.experimental.pallas import tpu as pltpu
from jax.sharding import PartitionSpec as P


EXPERTS_ALL = 384
CAP = 2
COLS, RINGS, CORES = 4, 16, 2
PAIRS = RINGS // 2
CHUNKS = 2
FIRST = 2
F32, BF16, I32 = jnp.float32, jnp.bfloat16, jnp.int32


def place(col, ring, core):
    return (col * RINGS + ring) * CORES + core


def pair_of(member, side):
    return (member + FIRST + 4 * side) & (PAIRS - 1)


def far_groups():
    groups = []
    for side in range(2):
        for core in range(CORES):
            members = []
            for col in range(COLS):
                for spot in range(PAIRS):
                    pair = pair_of(spot, side)
                    ring = 2 * pair + (side if pair < PAIRS // 2 else 1 - side)
                    members.append(place(col, ring, core))
            groups.append(members)
    return groups


FAR = far_groups()
MEMBERS = COLS * PAIRS
ROWS = MEMBERS * CAP
BESIDE = [(i, i ^ CORES) for i in range(COLS * RINGS * CORES)]
TWIN = [(i, i ^ 1) for i in range(COLS * RINGS * CORES)]
SLICE = EXPERTS_ALL // MEMBERS
RIDER = 128
TERMS = 3 * SLICE


def split3(v):
    a = v.astype(BF16)
    r = v - a.astype(F32)
    b = r.astype(BF16)
    c = (r - b.astype(F32)).astype(BF16)
    return a, b, c


def by_slice(e):
    return (e * 171) >> 11


def expert_of(member, side):
    return 2 * (member >> 3) + (pair_of(member, side) >> 2)


def slice_of(member, side):
    return (member & ~(PAIRS - 1)) + pair_of(member, side)


def iota(shape, axis):
    return lax.broadcasted_iota(I32, shape, axis)


def whole():
    return pl.BlockSpec(memory_space=pltpu.VMEM)


def scalar():
    return pl.BlockSpec(memory_space=pltpu.SMEM)


def pack_kernel(side_ref, tok_hbm, ids_hbm, score_hbm, out_ref, scale_ref, tok_ref, ids_ref, score_ref, flip_ids, flip_score, sems):
    fetch = pltpu.make_async_copy(tok_hbm, tok_ref, sems.at[0])
    small = [
        pltpu.make_async_copy(ids_hbm, ids_ref, sems.at[1]),
        pltpu.make_async_copy(score_hbm, score_ref, sems.at[2]),
    ]
    for copy in small + [fetch]:
        copy.start()
    side = side_ref[0]
    rows, width = tok_ref.shape
    top = ids_ref.shape[0]
    flip_ids[...] = jnp.zeros_like(flip_ids)
    flip_score[...] = jnp.zeros_like(flip_score)
    for copy in small:
        copy.wait()
    flip_ids[:top, :rows] = ids_ref[...]
    flip_score[:top, :rows] = score_ref[...]
    ids, score = flip_ids[...].T[:rows], flip_score[...].T[:rows]
    every = iota((rows, EXPERTS_ALL), 1)
    column = iota((rows, 128), 1)
    named = jnp.where(column < ROWS, expert_of(column >> 1, side), -1)
    mass = jnp.zeros((rows, EXPERTS_ALL), F32)
    gate = jnp.zeros((rows, 128), F32)
    hit = jnp.zeros((rows, 128), F32)
    for k in range(top):
        one, s = ids[:, k : k + 1], score[:, k : k + 1]
        mass = mass + jnp.where(every == one, s, 0.0)
        same = named == one
        gate = gate + jnp.where(same, s, 0.0)
        hit = hit + jnp.where(same, 1.0, 0.0)
    lower = jnp.where(iota((rows, rows), 0) >= iota((rows, rows), 1), 1.0, 0.0)
    rank = jnp.dot(lower.astype(BF16), hit.astype(BF16), preferred_element_type=F32) - 1.0
    slot = (column & 1).astype(F32)
    placed = (hit > 0.5) & (rank == slot)
    scale = split3(jnp.where(placed, gate, 0.0))
    for i, part in enumerate(scale):
        scale_ref[i * rows : (i + 1) * rows, :] = part
    pick = jnp.where(placed, 1.0, 0.0).T[:ROWS].astype(BF16)
    fetch.wait()
    picked = jnp.dot(pick, tok_ref[...], preferred_element_type=F32).astype(BF16)
    out_ref[:, :, :width] = picked.reshape(MEMBERS, CAP, width)
    load = jnp.sum(mass, axis=0, keepdims=True)
    row, e = iota((ROWS, EXPERTS_ALL), 0), iota((ROWS, EXPERTS_ALL), 1)
    mine = ((row & 1) == 0) & (slice_of(row >> 1, side) == by_slice(e))
    e2, lane = iota((EXPERTS_ALL, RIDER), 0), iota((EXPERTS_ALL, RIDER), 1)
    within = e2 - SLICE * by_slice(e2)
    rider = jnp.zeros((ROWS, RIDER), F32)
    for i, term in enumerate(split3(load)):
        spread = jnp.where(mine, term.astype(F32), 0.0).astype(BF16)
        select = jnp.where(lane == within + i * SLICE, 1.0, 0.0).astype(BF16)
        rider = rider + jnp.dot(spread, select, preferred_element_type=F32)
    out_ref[:, :, width:] = rider.astype(BF16).reshape(MEMBERS, CAP, RIDER)


def pack(side, tokens, ids, scores):
    rows, width = tokens.shape
    return pl.pallas_call(
        pack_kernel,
        out_shape=(
            jax.ShapeDtypeStruct((MEMBERS, CAP, width + RIDER), BF16),
            jax.ShapeDtypeStruct((3 * rows, 128), BF16),
        ),
        in_specs=[scalar()] + [pl.BlockSpec(memory_space=pl.ANY)] * 3,
        out_specs=(whole(), whole()),
        scratch_shapes=[
            pltpu.VMEM((rows, width), BF16),
            pltpu.VMEM(ids.shape[::-1], I32),
            pltpu.VMEM(scores.shape[::-1], F32),
            pltpu.VMEM((128, 128), I32),
            pltpu.VMEM((128, 128), F32),
            pltpu.SemaphoreType.DMA((3,)),
        ],
        compiler_params=pltpu.CompilerParams(vmem_limit_bytes=60 << 20),
        name="pack",
    )(side, tokens, ids.T, scores.T)


def expert_kernel(n_sums, x_ref, *refs):
    sums, mats, (out_ref, sum_ref) = refs[:n_sums], refs[n_sums : n_sums + 6], refs[n_sums + 6 :]
    width, hid = mats[0].shape
    rows = x_ref[...].reshape(-1, x_ref.shape[-1])
    x = rows[:, :width]
    total = jnp.sum(rows[:, width:].astype(F32), axis=0, keepdims=True)
    for other in sums:
        if other.shape[0] == 1:
            total = total + other[...]
        else:
            more = other[...].reshape(-1, other.shape[-1])[:, width:]
            total = total + jnp.sum(more.astype(F32), axis=0, keepdims=True)
    sum_ref[...] = total
    act = []
    for i in range(4):
        act.append(jnp.dot(x, mats[i][...], preferred_element_type=F32))
    g = jnp.concatenate(act[:2], axis=1)
    u = jnp.concatenate(act[2:], axis=1)
    h = (g / (1.0 + jnp.exp(-g)) * u).astype(BF16)
    out = [jnp.dot(h[:, i * hid : (i + 1) * hid], mats[4 + i][...], preferred_element_type=F32) for i in range(2)]
    out_ref[...] = (out[0] + out[1]).astype(out_ref.dtype)


def expert(x, sums, weights, twins, dtype):
    rows = x.shape[0] * CAP
    width, hid = weights[0].shape
    operands = [w for pair in zip(weights, twins) for w in pair]
    return pl.pallas_call(
        functools.partial(expert_kernel, len(sums)),
        out_shape=(jax.ShapeDtypeStruct((rows, width), dtype), jax.ShapeDtypeStruct((1, RIDER), F32)),
        in_specs=[whole()] * (7 + len(sums)),
        out_specs=(whole(), whole()),
        compiler_params=pltpu.CompilerParams(vmem_limit_bytes=14 << 20),
        cost_estimate=pl.CostEstimate(
            flops=12 * rows * width * hid, bytes_accessed=12 * width * hid, transcendentals=rows * 2 * hid
        ),
        name="expert",
    )(x, *sums, *operands)


def hold_kernel(*refs):
    n = len(refs) // 2
    sems = refs[-1]
    copies = [pltpu.make_async_copy(refs[i], refs[n + i], sems.at[i]) for i in range(n)]
    for copy in copies:
        copy.start()
    for copy in copies:
        copy.wait()


def hold(weights):
    return pl.pallas_call(
        hold_kernel,
        out_shape=tuple(jax.ShapeDtypeStruct(w.shape, w.dtype) for w in weights),
        in_specs=[pl.BlockSpec(memory_space=pl.ANY)] * len(weights),
        out_specs=(whole(),) * len(weights),
        scratch_shapes=[pltpu.SemaphoreType.DMA((len(weights),))],
        compiler_params=pltpu.CompilerParams(vmem_limit_bytes=4 << 20),
        name="hold",
    )(*weights)


def cut_kernel(whole_ref, *part_refs):
    many = part_refs[0].shape[0]
    for i, part in enumerate(part_refs):
        part[...] = whole_ref[pl.ds(i * many, many)]


def cut(blocks, pieces):
    shape = (blocks.shape[0] // pieces,) + blocks.shape[1:]
    return pl.pallas_call(
        cut_kernel,
        out_shape=(jax.ShapeDtypeStruct(shape, blocks.dtype),) * pieces,
        in_specs=[whole()],
        out_specs=(whole(),) * pieces,
        compiler_params=pltpu.CompilerParams(vmem_limit_bytes=3 << 20),
        name="cut",
    )(blocks)


def join_kernel(own_ref, sum_ref, twin_ref, *refs):
    backs, out_ref = refs[:-1], refs[-1]
    width = own_ref.shape[1]
    first = 0
    for back in backs:
        many = back.shape[0]
        both = (own_ref[pl.ds(first, many), :] + back[...].astype(F32)).astype(BF16)
        out_ref[pl.ds(first // CAP, many // CAP), :, :width] = both.reshape(many // CAP, CAP, width)
        first += many
    shape = (ROWS, RIDER)
    value = jnp.broadcast_to(sum_ref[...] + twin_ref[...], shape)
    keep = ((iota(shape, 0) & 1) == 0) & (iota(shape, 1) < TERMS)
    rider = jnp.zeros(shape, F32)
    for i, term in enumerate(split3(value)):
        term = jnp.where(keep, term.astype(F32), 0.0)
        rider = rider + (pltpu.roll(term, i * TERMS, 1) if i else term)
    out_ref[:, :, width:] = rider.astype(BF16).reshape(MEMBERS, CAP, RIDER)


def join(own, total, twin, backs):
    return pl.pallas_call(
        join_kernel,
        out_shape=jax.ShapeDtypeStruct((MEMBERS, CAP, own.shape[1] + RIDER), BF16),
        in_specs=[whole()] * (3 + len(backs)),
        out_specs=whole(),
        compiler_params=pltpu.CompilerParams(vmem_limit_bytes=8 << 20),
        name="join",
    )(own, total, twin, *backs)


def combine_kernel(side_ref, rows_ref, scale_ref, out_ref, mass_ref):
    side = side_ref[0]
    tok, width = out_ref.shape
    weight = scale_ref[:, :ROWS]
    rows = rows_ref[...].reshape(ROWS, -1)
    parts = jnp.dot(weight, rows[:, :width], preferred_element_type=F32)
    out_ref[...] = (parts[:tok] + parts[tok : 2 * tok] + parts[2 * tok :]).astype(BF16)
    lane, e = iota((RIDER, EXPERTS_ALL), 0), iota((RIDER, EXPERTS_ALL), 1)
    within = e - SLICE * by_slice(e)
    same = (lane - SLICE * by_slice(lane) == within) & (lane < 3 * TERMS)
    total = jnp.dot(rows[:, width:], jnp.where(same, 1.0, 0.0).astype(BF16), preferred_element_type=F32)
    row, e2 = iota((ROWS, EXPERTS_ALL), 0), iota((ROWS, EXPERTS_ALL), 1)
    mine = ((row & 1) == 0) & (slice_of(row >> 1, side) == by_slice(e2))
    mass_ref[...] = jnp.sum(jnp.where(mine, total, 0.0), axis=0)


def combine(side, rows, scale, tok):
    width = rows.shape[2] - RIDER
    return pl.pallas_call(
        combine_kernel,
        out_shape=(jax.ShapeDtypeStruct((tok, width), BF16), jax.ShapeDtypeStruct((EXPERTS_ALL,), F32)),
        in_specs=[scalar(), whole(), whole()],
        out_specs=(whole(), whole()),
        compiler_params=pltpu.CompilerParams(vmem_limit_bytes=6 << 20),
        name="combine",
    )(side, rows, scale)


def far(blocks):
    return lax.all_to_all(blocks, "exp", 0, 0, axis_index_groups=FAR, tiled=True)


def shards(tokens, expert_ids, gate_scores, gate_weight, up_weight, down_weight):
    tok_rows, _ = tokens.shape
    weights = (gate_weight, up_weight, down_weight)
    twins = tuple(lax.ppermute(w, "exp", TWIN) for w in weights)
    ring = (lax.axis_index("exp") // CORES) % RINGS
    side = ((ring & 1) ^ (ring >> 3)).astype(I32).reshape(1)
    out, scale = pack(side, tokens, expert_ids, gate_scores)
    mine = far(out)
    held = hold(weights)
    theirs = []
    for piece in cut(mine, CHUNKS):
        theirs.append(lax.ppermute(piece, "exp", BESIDE))
    backs, total = [], []
    for i, x in enumerate(theirs):
        partial, summed = expert(x, total + [mine] * (i == CHUNKS - 1), held, twins, BF16)
        backs.append(lax.ppermute(partial, "exp", BESIDE))
        total = [summed]
    own, _ = expert(mine, [], held, twins, F32)
    other = lax.ppermute(total[0], "exp", TWIN)
    returned = far(join(own, total[0], other, backs))
    combined, mass = combine(side, returned, scale, tok_rows)
    return combined, mass


def solution(mesh):
    return jax.shard_map(
        shards,
        mesh=mesh,
        in_specs=(
            P(("rep", "exp"), None),
            P(("rep", "exp"), None),
            P(("rep", "exp"), None),
            P(None, "exp"),
            P(None, "exp"),
            P("exp", None),
        ),
        out_specs=(P(("rep", "exp"), None), P("rep")),
        check_vma=False,
    )
```
